32 devices in a mesh: sec: 4 (over x, core), lat: 2 (over y), col: 4 (over z).
Axes of the slice: x: 2, y: 2, z: 4, core: 2. Of those that a mesh axis runs over, the one named last changes fastest.
Arguments:
- state: float32 [1, 4, 28, 192, 384], P(None, 'sec', None, 'lat', 'col'), may hold values from -6 to 6
- forcing: float32 [1, 4, 28, 192, 384], P(None, 'sec', None, 'lat', 'col'), may hold values from -4 to 4
- crm_moisture: bfloat16 [1, 32, 28, 8, 4, 2304], P(None, None, None, ('sec', 'lat'), 'col'), may hold values from -6 to 6
- cloud_order: int32 [4, 2, 9216], P('col', 'lat'), may hold values from 0 to 9215, each once within a row
- wave_table: int32 [128], replicated, may hold values from 0 to 127, each once
Outputs:
- state_out: float32 [1, 4, 28, 192, 384], P(None, 'sec', None, 'lat', 'col')
- spectral: float32 [4, 1, 28, 128, 2, 128], P('sec', None, 'col', 'lat')
The draws below stay inside these ranges and needn't reach their ends.
Inputs may be any that keep to these rules, and one draw needn't show every extreme that they name: `cloud_order`: every row lists each of the 9216 columns of a band block once. `wave_table`: each wavenumber stands in exactly one slot.
All inputs are finite; a program needn't handle non-finite values.
Results may differ from the reference program's by a relative error of at most 0.0003.
Values sent between devices are 32-bit elements; how exact they have to be, the bound alone decides.
A program may use at most 128 MiB of HBM per device.

```python
import math
import jax
import jax.numpy as jnp
from jax import lax

NLON = 384
NLAT = 192
L = 28
F = 4
MMAX = 128
NCRM = 32
NSUB = 4
ENS = 1
LON_BLOCK = 96
BLOCK_COLS = 9216
TARGETS = 8
PER_TARGET = 1152
RUN_COLS = 2304
N_LAT = 2
N_COL = 4


def block_levels(stream_key, dims, shards, least, top_value):
    def one(dim, blocks):
        draws = jax.random.uniform(jax.random.fold_in(jax.random.fold_in(stream_key, 6), dim), (blocks,), jnp.float32, least / len(shards), top_value / len(shards))
        return jnp.repeat(jnp.exp(draws), dims[dim] // blocks).reshape((-1,) + (1,) * (len(dims) - dim - 1))

    level = one(*shards[0])
    for cut in shards[1:]:
        level = level * one(*cut)
    return level


def normal_values(rng, dims, width, reach, shards=(), held_as=jnp.bfloat16):
    factor_of = block_levels(rng, dims, shards, -0.22, 0.18) if shards else 1.0
    values = jax.random.normal(rng, dims, jnp.float32) * width * factor_of
    return jnp.minimum(jnp.maximum(values, -reach), reach).astype(held_as)


def setup_inputs(seed: int = 0) -> dict:
    splits = jax.random.split(jax.random.key(seed), 6)
    state = normal_values(splits[0], (ENS, F, L, NLAT, NLON), 1.0, 6.0, ((1, 4), (3, 2), (4, 4)), jnp.float32)
    forcing = normal_values(splits[1], (ENS, F, L, NLAT, NLON), 0.5, 4.0, ((1, 4), (3, 2), (4, 4)), jnp.float32)
    crm_moisture = normal_values(splits[2], (ENS, NCRM, L, TARGETS, N_COL, RUN_COLS), 1.0, 6.0, ((3, 8), (4, 4)))
    cloud_order = jax.vmap(lambda own: jax.random.permutation(own, BLOCK_COLS))(jax.random.split(splits[3], N_COL * N_LAT)).reshape((N_COL, N_LAT, BLOCK_COLS)).astype(jnp.int32)
    wave_table = jax.random.permutation(splits[4], MMAX).astype(jnp.int32)
    return dict(state=state, forcing=forcing, crm_moisture=crm_moisture, cloud_order=cloud_order, wave_table=wave_table)


COURANT_SCALE = 0.4
CONDENSE = 0.5

def transport(values, courant, mixing):
    forward = jnp.roll(values, -1, axis=0)
    behind = jnp.roll(values, 1, axis=0)
    return -0.5 * courant * (forward - behind) + mixing * (forward - 2.0 * values + behind)

def cloud_model(vertical_state_stack, forcing, vapour_mass_fraction):
    wind_u = vertical_state_stack[0]
    wind_v = vertical_state_stack[1]
    atmospheric_warmth = vertical_state_stack[2]
    humidity = vertical_state_stack[3]
    courant = COURANT_SCALE * jnp.tanh(wind_u)
    mixing = 0.2 + 0.5 * jnp.abs(courant)
    convective_warming_rate = jnp.broadcast_to(atmospheric_warmth, vapour_mass_fraction.shape)
    crm_water = humidity + vapour_mass_fraction
    start_water = crm_water
    ground_precipitation = jnp.zeros_like(atmospheric_warmth)
    for substep in range(NSUB):
        heat_move = transport(convective_warming_rate, courant, mixing)
        water_move = transport(crm_water, courant, mixing)
        condensed = CONDENSE * jnp.maximum(crm_water - convective_warming_rate, 0.0)
        convective_warming_rate = convective_warming_rate + heat_move + condensed + forcing[2] / NSUB
        crm_water = crm_water + water_move - condensed + forcing[3] / NSUB
        ground_precipitation = ground_precipitation + lax.optimization_barrier(jnp.mean(condensed, axis=0))
    ground_precipitation = ground_precipitation / NSUB
    zonal_velocity_rate = -ground_precipitation * wind_u + forcing[0]
    meridional_velocity_rate = -ground_precipitation * wind_v + forcing[1]
    warming_rate_change = lax.optimization_barrier(jnp.mean(convective_warming_rate, axis=0)) - atmospheric_warmth
    vapour_rate_change = lax.optimization_barrier(jnp.mean(crm_water - start_water, axis=0))
    return jnp.stack((zonal_velocity_rate, meridional_velocity_rate, warming_rate_change, vapour_rate_change))

def trig_table(longitudes, wave_numbers):
    phase = (longitudes[:, None] * wave_numbers[None, :] % NLON).astype(jnp.float32) * (2.0 * math.pi / NLON)
    return jnp.stack((jnp.cos(phase), jnp.sin(phase)), axis=1) / math.sqrt(NLON)

def legendre_table(orders):
    colatitude = (jnp.arange(NLAT, dtype=jnp.int32).astype(jnp.float32) + 0.5) * (math.pi / NLAT)
    cosine = jnp.cos(colatitude)[None, :]
    sine_lat = jnp.sin(colatitude)
    order_col = orders.astype(jnp.float32)[:, None]
    log_diag = 0.5 * (lax.lgamma(order_col + 1.5) - lax.lgamma(jnp.float32(1.5)) - lax.lgamma(order_col + 1.0))
    log_diag = log_diag + order_col * jnp.log(sine_lat)[None, :] - 0.5 * math.log(2.0)
    diagonal = jnp.exp(log_diag)
    empty = jnp.zeros_like(diagonal)

    def march_forward(carried, degree):
        previous, current = carried
        deg_float = degree.astype(jnp.float32)
        active = deg_float > order_col
        numerator = jnp.where(active, 4.0 * deg_float * deg_float - 1.0, 1.0)
        bottom = jnp.where(active, deg_float * deg_float - order_col * order_col, 1.0)
        lower_deg = deg_float - 1.0
        retreat = jnp.sqrt(jnp.maximum(lower_deg * lower_deg - order_col * order_col, 0.0) / (4.0 * lower_deg * lower_deg - 1.0))
        grown = jnp.sqrt(numerator / bottom) * (cosine * current - retreat * previous)
        fresh_row = jnp.where(active, grown, jnp.where(deg_float == order_col, diagonal, 0.0))
        return ((current, fresh_row), fresh_row)
    _, legendre_rows = lax.scan(march_forward, (empty, empty), jnp.arange(MMAX, dtype=jnp.int32), unroll=8)
    weights = sine_lat / math.sqrt(NLAT)
    return legendre_rows * weights[None, None, :]

def reference(state, forcing, crm_moisture, cloud_order, wave_table):
    updated = []
    for member in range(ENS):
        member_state = state[member]
        member_force = forcing[member]
        member_moist = crm_moisture[member]

        def per_group(col_group):
            lon_start = col_group * LON_BLOCK
            grid_block = lax.dynamic_slice_in_dim(member_state, lon_start, LON_BLOCK, 3).reshape(F, L, N_LAT, BLOCK_COLS)
            force_block = lax.dynamic_slice_in_dim(member_force, lon_start, LON_BLOCK, 3).reshape(F, L, N_LAT, BLOCK_COLS)
            col_order = lax.dynamic_index_in_dim(cloud_order, col_group, 0, keepdims=False)

            def to_slots(values):
                chosen = jnp.take_along_axis(values, jnp.broadcast_to(col_order[None, None], values.shape), axis=3)
                chosen = chosen.reshape(F, L, N_LAT, TARGETS, PER_TARGET).transpose(0, 1, 3, 2, 4)
                return chosen.reshape(F, L, TARGETS * RUN_COLS)
            vapour_mass_fraction = lax.dynamic_index_in_dim(member_moist, col_group, 3, keepdims=False)
            vapour_mass_fraction = vapour_mass_fraction.astype(jnp.float32).reshape(NCRM, L, TARGETS * RUN_COLS)
            tendencies = cloud_model(to_slots(grid_block), to_slots(force_block), vapour_mass_fraction)
            tendencies = tendencies.reshape(F, L, TARGETS, N_LAT, PER_TARGET).transpose(0, 1, 3, 2, 4)
            tendencies = tendencies.reshape(F, L, N_LAT, BLOCK_COLS)
            inverse = jnp.argsort(col_order, axis=1).astype(jnp.int32)
            restored = jnp.take_along_axis(tendencies, jnp.broadcast_to(inverse[None, None], tendencies.shape), axis=3)
            return restored.reshape(F, L, NLAT, LON_BLOCK)
        pieces = lax.map(per_group, jnp.arange(N_COL, dtype=jnp.int32))
        column_tend = pieces.transpose(1, 2, 3, 0, 4).reshape(F, L, NLAT, NLON)
        updated.append(member_state + column_tend)
    new_state = jnp.stack(updated)
    trig_rows = trig_table(jnp.arange(NLON, dtype=jnp.int32), wave_table)
    fourier = jnp.einsum('eflay,ycs->eflacs', new_state, trig_rows, precision=lax.Precision.HIGHEST)
    weighted = legendre_table(wave_table)
    spectral = jnp.einsum('eflacs,nsa->felscn', fourier, weighted, precision=lax.Precision.HIGHEST)
    return (new_state, spectral)
```

```python
import math

import jax
import jax.numpy as jnp
from jax import lax
from jax.experimental import pallas as pl
from jax.experimental.pallas import tpu as pltpu
from jax.sharding import PartitionSpec as P

NLON = 384
NLAT = 192
MMAX = 128
NSUB = 4
LANES = 128
ROWS = 8

COURANT_SCALE = 0.4
CONDENSE = 0.5


def permute_kernel(x_ref, order_ref, out_ref, parts, held):
    levels = x_ref.shape[-2]
    rows = held.shape[0]
    cols = order_ref.shape[1]
    tiles = cols // LANES
    gathered = held.shape[1] // LANES
    multiplied = tiles - gathered
    halves = 2 if tiles % 2 == 0 else 1
    width = halves * LANES
    fill = jnp.zeros((rows - levels, LANES), jnp.float32)
    groups = range(rows // ROWS)

    for s in range(tiles):
        if x_ref.ndim == 2:
            block = x_ref[:, s * LANES : (s + 1) * LANES]
        else:
            per = x_ref.shape[2] // LANES
            block = x_ref[s // per, :, s % per * LANES : (s % per + 1) * LANES]
        if rows > levels:
            block = jnp.concatenate([block, fill], axis=0)
        if s < multiplied:
            coarse = block.astype(jnp.bfloat16)
            parts[s * rows : (s + 1) * rows, :LANES] = coarse
            parts[s * rows : (s + 1) * rows, LANES:] = (
                block - coarse.astype(jnp.float32)
            ).astype(jnp.bfloat16)
        else:
            held[:, (s - multiplied) * LANES : (s - multiplied + 1) * LANES] = block
    wanted = lax.broadcasted_iota(jnp.int32, (2 * LANES, width), 0) & (LANES - 1)

    def one(t, carry):
        order = order_ref[:, pl.ds(pl.multiple_of(t * width, width), width)]
        lane = order & (LANES - 1)
        chosen = jnp.where(wanted == lane, 1.0, 0.0).astype(jnp.bfloat16)
        moved = jnp.dot(parts[...], chosen, preferred_element_type=jnp.float32)
        for h in range(halves):
            mine = slice(h * LANES, (h + 1) * LANES)
            source = jnp.broadcast_to(order[:, mine] >> 7, (ROWS, LANES))
            lanes = jnp.broadcast_to(lane[:, mine], (ROWS, LANES))
            total = [jnp.zeros((ROWS, LANES), jnp.float32) for _ in groups]
            for s in range(gathered):
                hit = source == multiplied + s
                for r in groups:
                    block = held[r * ROWS : (r + 1) * ROWS, s * LANES : (s + 1) * LANES]
                    total[r] = jnp.where(hit, jnp.take_along_axis(block, lanes, axis=1), total[r])
            for s in range(multiplied):
                hit = source == s
                for r in groups:
                    begin = s * rows + r * ROWS
                    total[r] = jnp.where(hit, moved[begin : begin + ROWS, mine], total[r])
            tile = t * halves + h
            for r in groups:
                end = min((r + 1) * ROWS, levels)
                value = total[r][: end - r * ROWS]
                if out_ref.ndim == 2:
                    at = pl.ds(pl.multiple_of(tile * LANES, LANES), LANES)
                    out_ref[r * ROWS : end, at] = value
                else:
                    per = out_ref.shape[2] // LANES
                    at = pl.ds(pl.multiple_of(tile % per * LANES, LANES), LANES)
                    out_ref[tile // per, r * ROWS : end, at] = value
        return carry

    lax.fori_loop(0, tiles // halves, one, 0)


def permute(values, order, shape):
    levels, tiles = values.shape[-2], order.shape[1] // LANES
    rows = -(-levels // ROWS) * ROWS
    gathered = tiles * 3 // 8
    return pl.pallas_call(
        permute_kernel,
        out_shape=jax.ShapeDtypeStruct(shape, jnp.float32),
        in_specs=[pl.BlockSpec(memory_space=pltpu.VMEM)] * 2,
        out_specs=pl.BlockSpec(memory_space=pltpu.VMEM),
        scratch_shapes=[
            pltpu.VMEM(((tiles - gathered) * rows, 2 * LANES), jnp.bfloat16),
            pltpu.VMEM((rows, gathered * LANES), jnp.float32),
        ],
        name="permute",
    )(values, order)


def cloud_kernel(wind_ref, gap_ref, push_ref, anomaly_ref, rain_ref):
    count, levels, width = anomaly_ref.shape
    scale = CONDENSE / count

    for c0 in range(0, width, LANES):
        c1 = min(c0 + LANES, width)
        for base in range(0, levels, 2 * ROWS):
            top = min(base + 2 * ROWS, levels)
            for r0 in range(base, top, ROWS):
                r1 = min(r0 + ROWS, top)
                courant = COURANT_SCALE * jnp.tanh(wind_ref[r0:r1, c0:c1])
                mixing = 0.2 + 0.5 * jnp.abs(courant)
                ahead = mixing - 0.5 * courant
                back = mixing + 0.5 * courant
                keep = 1.0 - 2.0 * mixing
                push = push_ref[r0:r1, c0:c1]
                start = gap_ref[r0:r1, c0:c1]
                gap = [
                    start
                    + anomaly_ref[n, base:top, c0:c1].astype(jnp.float32)[r0 - base : r1 - base]
                    for n in range(count)
                ]
                rain = [jnp.zeros_like(start) for _ in range(2)]
                for substep in range(NSUB):
                    fresh = []
                    for n in range(count):
                        wet = jnp.maximum(gap[n], 0.0)
                        rain[n % 2] = rain[n % 2] + wet
                        if substep < NSUB - 1:
                            fresh.append(
                                (ahead * gap[(n + 1) % count] + back * gap[n - 1])
                                + (keep * gap[n] + (push - wet))
                            )
                    gap = fresh
                found = scale * (rain[0] + rain[1])
                for copy in range(rain_ref.shape[0]):
                    rain_ref[copy, r0:r1, c0:c1] = found


def cloud_model(arrived, anomaly, sections):
    count, levels, _ = anomaly.shape
    blocks, _, span = arrived.shape
    bands = blocks // sections
    block = LANES if span % LANES == 0 else span
    steps = span // block
    if block < LANES:
        anomaly = anomaly.reshape(count, levels, bands, span).transpose(2, 0, 1, 3)
        moist = pl.BlockSpec((None, count, levels, span), lambda i: (i, 0, 0, 0))
    else:
        moist = pl.BlockSpec((count, levels, block), lambda i: (0, 0, i))

    def of(field):
        return pl.BlockSpec(
            (None, levels, block), lambda i: (field * bands + i // steps, 0, i % steps)
        )

    found = pl.pallas_call(
        cloud_kernel,
        grid=(bands * steps,),
        out_shape=jax.ShapeDtypeStruct((sections, bands, levels, span), jnp.float32),
        in_specs=[of(0), of(2), of(3), moist],
        out_specs=pl.BlockSpec(
            (sections, None, levels, block), lambda i: (0, i // steps, 0, i % steps)
        ),
        name="cloud",
    )(arrived, arrived, arrived, anomaly)
    return found.reshape(arrived.shape)


def halve(values):
    coarse = values.astype(jnp.bfloat16)
    return coarse, (values - coarse.astype(jnp.float32)).astype(jnp.bfloat16)


def march_kernel(
    grow_ref, retreat_ref, order_ref, zero_ref, cosine_ref, diag_ref, coarse_ref, fine_ref, *tables
):
    slots = order_ref.shape[0]
    halves = len(tables)
    order = order_ref[...]
    grow = grow_ref[...]
    retreat = retreat_ref[...]
    cosine = [cosine_ref[:, h * LANES : (h + 1) * LANES] for h in range(halves)]
    for h in range(halves):
        tables[h][: 2 * slots, :] = jnp.zeros((2 * slots, LANES), jnp.float32)
    group = 8

    def march(g, carry):
        begin = g * group
        held = [
            [
                tables[h][pl.ds(pl.multiple_of((begin + j) * slots, ROWS), slots), :]
                for j in range(2)
            ]
            for h in range(halves)
        ]
        for j in range(group):
            n = begin + j
            index = zero_ref[...] + n
            grow_n = jnp.take_along_axis(grow, index, axis=1)
            retreat_n = jnp.take_along_axis(retreat, index, axis=1)
            first = order == n
            for h in range(halves):
                previous, current = held[h]
                grown = grow_n * (cosine[h] * current - retreat_n * previous)
                fresh = jnp.where(first, diag_ref[:, h * LANES : (h + 1) * LANES], grown)
                tables[h][pl.ds(pl.multiple_of((n + 2) * slots, ROWS), slots), :] = fresh
                held[h] = [current, fresh]
        return carry

    lax.fori_loop(0, MMAX // group, march, 0)

    def sort(g, carry):
        for j in range(4):
            s = g * 4 + j
            for h in range(halves):
                rows = tables[h][pl.ds(2 * slots + s, MMAX, stride=slots), :]
                mine = slice(h * LANES, (h + 1) * LANES)
                coarse_ref[s, :, mine], fine_ref[s, :, mine] = halve(rows)
        return carry

    lax.fori_loop(0, slots // 4, sort, 0)


def contract_kernel(fourier_ref, coarse_ref, fine_ref, out_ref):
    levels, slots, _, _ = out_ref.shape
    bands = fourier_ref.shape[0]
    terms = 2 * levels
    rows = -(-terms // 16) * 16

    def product(left, right):
        return lax.dot_general(
            left, right, (((1,), (1,)), ((), ())), preferred_element_type=jnp.float32
        )

    def contract(g, carry):
        for j in range(4):
            s = g * 4 + j
            found = [fourier_ref[b, pl.ds(s, terms, stride=slots), :] for b in range(bands)]
            found = jnp.concatenate(found, axis=1)
            if rows > terms:
                fill = jnp.zeros((rows - terms, found.shape[1]), jnp.float32)
                found = jnp.concatenate([found, fill], axis=0)
            head, rest = halve(found)
            main = product(jnp.concatenate([head, rest], axis=0), coarse_ref[s])
            total = main[:rows] + main[rows:] + product(head, fine_ref[s])
            for l in range(levels):
                out_ref[l, s] = total[2 * l : 2 * l + 2]
        return carry

    lax.fori_loop(0, slots // 4, contract, 0)


def dft_kernel(x_ref, trig_ref, out_ref):
    blocks, levels, lats, _ = x_ref.shape
    parts, _, _, slots, lanes = out_ref.shape
    count = trig_ref.shape[1]
    waves = [jnp.concatenate(halve(trig_ref[j]), axis=0) for j in range(blocks)]

    def product(left, right):
        return lax.dot_general(
            left, right, (((1,), (1,)), ((), ())), preferred_element_type=jnp.float32
        )

    for first in range(0, levels, 2):
        last = min(first + 2, levels)
        total = None
        for j in range(blocks):
            grid = []
            for l in range(first, last):
                grid.append(x_ref[j, l])
                if lanes > lats:
                    grid.append(jnp.zeros((lanes - lats, x_ref.shape[3]), jnp.float32))
            coarse, fine = halve(jnp.concatenate(grid, axis=0))
            main = product(waves[j], coarse)
            term = main[:count] + main[count:] + product(waves[j][:count], fine)
            total = term if total is None else total + term
        for l in range(first, last):
            mine = total[:, (l - first) * lanes : (l - first + 1) * lanes]
            for p in range(parts):
                for c in range(2):
                    begin = (p * 2 + c) * slots
                    out_ref[p, l, c] = mine[begin : begin + slots]


def dft(regrouped, wave_table, blocks, parts):
    _, lats, lons = regrouped.shape
    levels = regrouped.shape[0] // blocks
    slots = wave_table.shape[0] // parts
    pad = -lats % ROWS
    lanes = -(-lats // LANES) * LANES
    grid = jnp.pad(regrouped, ((0, 0), (0, pad), (0, 0)))
    trig = trig_table(jnp.arange(NLON, dtype=jnp.int32), wave_table)
    trig = trig.reshape(blocks, lons, 2, parts, slots).transpose(0, 3, 2, 4, 1)
    return pl.pallas_call(
        dft_kernel,
        out_shape=jax.ShapeDtypeStruct((parts, levels, 2, slots, lanes), jnp.float32),
        in_specs=[pl.BlockSpec(memory_space=pltpu.VMEM)] * 2,
        out_specs=pl.BlockSpec(memory_space=pltpu.VMEM),
        name="dft",
    )(
        grid.reshape(blocks, levels, lats + pad, lons),
        trig.reshape(blocks, 2 * parts * slots, lons),
    )


def legendre_terms(orders, lats):
    colatitude = (jnp.arange(lats, dtype=jnp.int32).astype(jnp.float32) + 0.5) * (math.pi / lats)
    sine_lat = jnp.sin(colatitude)
    order_col = orders.astype(jnp.float32)[:, None]
    log_diag = 0.5 * (
        lax.lgamma(order_col + 1.5) - lax.lgamma(jnp.float32(1.5)) - lax.lgamma(order_col + 1.0)
    )
    log_diag = log_diag + order_col * jnp.log(sine_lat)[None, :] - 0.5 * math.log(2.0)
    diagonal = jnp.exp(log_diag) * (sine_lat / math.sqrt(lats))[None, :]
    degree = jnp.arange(MMAX, dtype=jnp.int32).astype(jnp.float32)[None, :]
    active = degree > order_col
    numerator = jnp.where(active, 4.0 * degree * degree - 1.0, 0.0)
    bottom = jnp.where(active, degree * degree - order_col * order_col, 1.0)
    lower = degree - 1.0
    retreat = jnp.sqrt(
        jnp.maximum(lower * lower - order_col * order_col, 0.0) / (4.0 * lower * lower - 1.0)
    )
    return jnp.sqrt(numerator / bottom), retreat, jnp.cos(colatitude), diagonal


def legendre_tables(orders, lats, bands):
    slots = orders.shape[0]
    wide = bands * (-(-(lats // bands) // LANES) * LANES)
    grow, retreat, cosine, diagonal = legendre_terms(orders, lats)

    def spread(values):
        cut = values.reshape(values.shape[0], bands, lats // bands)
        cut = jnp.pad(cut, ((0, 0), (0, 0), (0, wide // bands - lats // bands)))
        return cut.reshape(values.shape[0], wide)

    table = jax.ShapeDtypeStruct((slots, MMAX, wide), jnp.bfloat16)
    return pl.pallas_call(
        march_kernel,
        out_shape=[table] * 2,
        in_specs=[pl.BlockSpec(memory_space=pltpu.VMEM)] * 6,
        out_specs=[pl.BlockSpec(memory_space=pltpu.VMEM)] * 2,
        scratch_shapes=[pltpu.VMEM(((MMAX + 2) * slots, LANES), jnp.float32)] * (wide // LANES),
        cost_estimate=pl.CostEstimate(
            flops=6 * MMAX * slots * wide, bytes_accessed=16 * MMAX * slots * wide, transcendentals=0
        ),
        name="march",
    )(
        grow,
        retreat,
        jnp.broadcast_to(orders[:, None], (slots, LANES)),
        jnp.zeros((slots, LANES), jnp.int32),
        spread(cosine[None, :]),
        spread(diagonal),
    )


def contract_tables(fourier, tables):
    bands, levels, _, slots, lanes = fourier.shape
    return pl.pallas_call(
        contract_kernel,
        out_shape=jax.ShapeDtypeStruct((levels, slots, 2, MMAX), jnp.float32),
        in_specs=[pl.BlockSpec(memory_space=pltpu.VMEM)] * 3,
        out_specs=pl.BlockSpec(memory_space=pltpu.VMEM),
        name="contract",
    )(fourier.reshape(bands, levels * 2 * slots, lanes), *tables)


def trig_table(longitudes, wave_numbers):
    phase = (longitudes[:, None] * wave_numbers[None, :] % NLON).astype(jnp.float32) * (
        2.0 * math.pi / NLON
    )
    return jnp.stack((jnp.cos(phase), jnp.sin(phase)), axis=1) / math.sqrt(NLON)


MESH_IDS = pl.DeviceIdType.MESH


def lanes_product(left, right):
    return lax.dot_general(
        left, right, (((1,), (1,)), ((), ())), preferred_element_type=jnp.float32
    )


def march(grow, retreat, order, zero, cosine, diag_ref, table, coarse_ref, fine_ref):
    slots = order.shape[0]
    table[: 2 * slots, :] = jnp.zeros((2 * slots, LANES), jnp.float32)
    group = 8

    def degrees(g, carry):
        begin = g * group
        previous, current = [
            table[pl.ds(pl.multiple_of((begin + j) * slots, ROWS), slots), :] for j in range(2)
        ]
        for j in range(group):
            n = begin + j
            index = zero + n
            grow_n = jnp.take_along_axis(grow, index, axis=1)
            retreat_n = jnp.take_along_axis(retreat, index, axis=1)
            grown = grow_n * (cosine * current - retreat_n * previous)
            fresh = jnp.where(order == n, diag_ref[...], grown)
            table[pl.ds(pl.multiple_of((n + 2) * slots, ROWS), slots), :] = fresh
            previous, current = current, fresh
        return carry

    lax.fori_loop(0, MMAX // group, degrees, 0)

    def sort(g, carry):
        for j in range(4):
            s = g * 4 + j
            rows = table[pl.ds(2 * slots + s, MMAX, stride=slots), :]
            coarse_ref[s], fine_ref[s] = halve(rows)
        return carry

    lax.fori_loop(0, slots // 4, sort, 0)


def spectral_kernel(
    fresh_ref,
    trig_ref,
    grow_ref,
    retreat_ref,
    order_ref,
    zero_ref,
    cosine_ref,
    diag_ref,
    out_ref,
    zbuf,
    ybuf,
    ystage,
    wave_coarse,
    wave_fine,
    table,
    coarse,
    fine,
    both,
    local_sem,
    zsend,
    zrecv,
    ysend,
    yrecv,
):
    cols = lax.axis_size("col")
    col, lat = lax.axis_index("col"), lax.axis_index("lat")
    levels, lats = zbuf.shape[1], zbuf.shape[2]
    slots = order_ref.shape[0]
    partner = 1 - lat

    barrier = pltpu.get_barrier_semaphore()
    for d in range(1, cols):
        pl.semaphore_signal(
            barrier, inc=1, device_id={"col": lax.rem(col + d, cols)}, device_id_type=MESH_IDS
        )
    pl.semaphore_signal(barrier, inc=1, device_id={"lat": partner}, device_id_type=MESH_IDS)
    own = pltpu.make_async_copy(
        fresh_ref.at[pl.ds(col * levels, levels)], zbuf.at[col], local_sem
    )
    own.start()
    pl.semaphore_wait(barrier, cols)

    def zcopy(l, d):
        dest = lax.rem(col + d, cols)
        return pltpu.make_async_remote_copy(
            src_ref=fresh_ref.at[dest * levels + l],
            dst_ref=zbuf.at[col, l],
            send_sem=zsend.at[l, d - 1],
            recv_sem=zrecv.at[l, d - 1],
            device_id={"col": dest},
            device_id_type=MESH_IDS,
        )

    for l in range(levels):
        for d in range(1, cols):
            zcopy(l, d).start()

    for j in range(cols):
        wave_coarse[j], wave_fine[j] = halve(trig_ref[j])
    march(
        grow_ref[...],
        retreat_ref[...],
        order_ref[...],
        zero_ref[...],
        cosine_ref[...],
        diag_ref,
        table,
        coarse,
        fine,
    )
    own.wait()

    def ycopy(l):
        return pltpu.make_async_remote_copy(
            src_ref=ystage.at[l],
            dst_ref=ybuf.at[lat, l],
            send_sem=ysend.at[l],
            recv_sem=yrecv.at[l],
            device_id={"lat": partner},
            device_id_type=MESH_IDS,
        )

    def transform(l, carry):
        for d in range(1, cols):
            zcopy(l, d).wait_recv()
        total = None
        for j in range(cols):
            head, rest = halve(zbuf[j, l])
            main = lanes_product(jnp.concatenate([head, rest], axis=0), wave_coarse[j])
            term = main[:lats] + main[lats:] + lanes_product(head, wave_fine[j])
            total = term if total is None else total + term
        ybuf[lat, l] = total[:, : 2 * slots]
        ystage[l] = total[:, 2 * slots :]
        ycopy(l).start()
        return carry

    lax.fori_loop(0, levels, transform, 0)

    lane = lax.broadcasted_iota(jnp.int32, (2 * slots, LANES), 1)
    mirror = jnp.where(lane < lats, lats - 1 - lane, lane)
    fill = jnp.zeros((2 * slots, LANES - lats), jnp.float32)
    both[...] = jnp.zeros_like(both)
    span = both.shape[0] // 2

    def mix(l, carry):
        ycopy(l).wait_recv()
        north = jnp.concatenate([ybuf[0, l].T, fill], axis=1)
        south = jnp.concatenate([ybuf[1, l].T, fill], axis=1)
        south = jnp.take_along_axis(south, mirror, axis=1)
        at = pl.ds(pl.multiple_of(l * 2 * slots, ROWS), 2 * slots)
        both[at, :] = north + south
        at = pl.ds(pl.multiple_of(span + l * 2 * slots, ROWS), 2 * slots)
        both[at, :] = north - south
        return carry

    lax.fori_loop(0, levels, mix, 0)
    half = both.shape[0] // slots // 2
    degree = lax.broadcasted_iota(jnp.int32, (half, LANES), 1)

    def contract(g, carry):
        for j in range(4):
            s = g * 4 + j
            head, rest = halve(both[pl.ds(s, 2 * half, stride=slots), :])
            main = lanes_product(jnp.concatenate([head, rest], axis=0), coarse[s])
            total = main[: 2 * half] + main[2 * half :] + lanes_product(head, fine[s])
            even = ((order_ref[pl.ds(s, 1), :] + degree) & 1) == 0
            total = jnp.where(even, total[:half], total[half:])
            for l in range(levels):
                out_ref[l, s] = total[2 * l : 2 * l + 2]
        return carry

    lax.fori_loop(0, slots // 4, contract, 0)

    def drain(l, carry):
        for d in range(1, cols):
            zcopy(l, d).wait_send()
        ycopy(l).wait_send()
        return carry

    lax.fori_loop(0, levels, drain, 0)


def spectral_step(fresh, wave_table):
    cols, lat_bands = lax.axis_size("col"), lax.axis_size("lat")
    total_levels, band_rows, lon_block = fresh.shape
    levels = total_levels // cols
    slots = MMAX // lat_bands
    lat = lax.axis_index("lat")
    waves = lax.dynamic_slice_in_dim(
        jnp.concatenate([wave_table, wave_table]), lat * slots, lat_bands * slots
    )
    trig = trig_table(jnp.arange(NLON, dtype=jnp.int32), waves)
    trig = trig.reshape(cols, lon_block, 2, lat_bands, slots).transpose(0, 3, 2, 4, 1)
    trig = trig.reshape(cols, lat_bands * 2 * slots, lon_block)
    grow, retreat, cosine, diagonal = legendre_terms(waves[:slots], NLAT)
    pad = ((0, 0), (0, LANES - band_rows))
    vmem = pl.BlockSpec(memory_space=pltpu.VMEM)
    half = -(-2 * levels // ROWS) * ROWS
    return pl.pallas_call(
        spectral_kernel,
        out_shape=jax.ShapeDtypeStruct((levels, slots, 2, MMAX), jnp.float32),
        in_specs=[pl.BlockSpec(memory_space=pl.ANY)] + [vmem] * 7,
        out_specs=vmem,
        scratch_shapes=[
            pltpu.VMEM((cols, levels, band_rows, lon_block), jnp.float32),
            pltpu.VMEM((lat_bands, levels, band_rows, 2 * slots), jnp.float32),
            pltpu.VMEM((levels, band_rows, 2 * slots), jnp.float32),
            pltpu.VMEM(trig.shape, jnp.bfloat16),
            pltpu.VMEM(trig.shape, jnp.bfloat16),
            pltpu.VMEM(((MMAX + 2) * slots, LANES), jnp.float32),
            pltpu.VMEM((slots, MMAX, LANES), jnp.bfloat16),
            pltpu.VMEM((slots, MMAX, LANES), jnp.bfloat16),
            pltpu.VMEM((2 * half * slots, LANES), jnp.float32),
            pltpu.SemaphoreType.DMA,
            pltpu.SemaphoreType.DMA((levels, cols - 1)),
            pltpu.SemaphoreType.DMA((levels, cols - 1)),
            pltpu.SemaphoreType.DMA((levels,)),
            pltpu.SemaphoreType.DMA((levels,)),
        ],
        compiler_params=pltpu.CompilerParams(collective_id=1, has_side_effects=True),
        name="spectral",
    )(
        fresh,
        trig,
        grow,
        retreat,
        jnp.broadcast_to(waves[:slots, None], (slots, LANES)),
        jnp.zeros((slots, LANES), jnp.int32),
        jnp.pad(cosine[None, :band_rows], pad),
        jnp.pad(diagonal[:, :band_rows], pad),
    )


def inverse_order(order):
    cols = order.shape[0]
    tiles = cols // LANES
    slots = jnp.arange(cols, dtype=jnp.int32)
    high = (order[None, :] // LANES) == jnp.arange(tiles, dtype=jnp.int32)[:, None]
    low = (order[:, None] % LANES) == jnp.arange(LANES, dtype=jnp.int32)[None, :]
    digits = jnp.stack((slots // LANES, slots % LANES)).astype(jnp.bfloat16)
    left = jnp.where(high[None], digits[:, None, :], jnp.bfloat16(0)).reshape(2 * tiles, cols)
    found = jnp.dot(left, low.astype(jnp.bfloat16), preferred_element_type=jnp.float32)
    found = found.reshape(2, cols).astype(jnp.int32)
    return found[0] * LANES + found[1]


def shards(state, forcing, crm_moisture, cloud_order, wave_table):
    members, _, levels, band_rows, lon_block = state.shape
    sections = lax.axis_size("sec")
    lat_bands = lax.axis_size("lat")
    block_cols = band_rows * lon_block
    targets = sections * lat_bands
    per_target = block_cols // targets
    field = lax.axis_index("sec")
    slot_list = cloud_order[0, 0]
    own, force = state[0, 0], forcing[0, 0]

    mate = lax.ppermute(jnp.where(field == 2, force, own), "sec", [(2, 3), (3, 2)])
    part = jnp.where(
        field == 3, (force - mate) / NSUB, jnp.where(field == 2, mate - own, own)
    )
    flat = part.reshape(levels, block_cols)
    cut = (targets, levels, per_target)
    tiled = per_target % LANES == 0
    if tiled:
        outgoing = permute(flat, slot_list[None, :], cut)
    else:
        in_slots = permute(flat, slot_list[None, :], flat.shape)
        outgoing = in_slots.reshape(levels, targets, per_target).transpose(1, 0, 2)
    crm_moisture, outgoing = lax.optimization_barrier((crm_moisture, outgoing))
    arrived = lax.all_to_all(outgoing, ("sec", "lat"), split_axis=0, concat_axis=0, tiled=True)
    homeward = cloud_model(arrived, crm_moisture[0, :, :, 0, 0, :], sections)
    returned = lax.all_to_all(homeward, ("sec", "lat"), split_axis=0, concat_axis=0, tiled=True)
    if not tiled:
        returned = returned.transpose(1, 0, 2).reshape(levels, block_cols)
    rainfall = permute(returned, inverse_order(slot_list)[None, :], flat.shape)
    rainfall = rainfall.reshape(levels, band_rows, lon_block)
    share = jnp.where(
        field < 2, own * (-1.0 / NSUB), jnp.where(field == 2, jnp.float32(1), jnp.float32(-1))
    )
    fresh = own + (share * rainfall + force)

    whole_lanes = 2 * MMAX // lat_bands == LANES and band_rows <= LANES
    if lat_bands == 2 and whole_lanes and levels % lax.axis_size("col") == 0:
        coeffs = spectral_step(fresh, wave_table)
        return (fresh[None, None], coeffs[None, None])

    regrouped = lax.all_to_all(fresh, "col", split_axis=0, concat_axis=0, tiled=True)
    owner_count = MMAX // lat_bands
    wave_table, _ = lax.optimization_barrier((wave_table, rainfall))
    owned_waves = lax.dynamic_slice_in_dim(
        wave_table, lax.axis_index("lat") * owner_count, owner_count
    )
    tables = legendre_tables(owned_waves, NLAT, lat_bands)
    regrouped, tables = lax.optimization_barrier((regrouped, tables))
    spectra = dft(regrouped, wave_table, lax.axis_size("col"), lat_bands)
    gathered = lax.all_to_all(spectra, "lat", split_axis=0, concat_axis=0, tiled=True)
    coeffs = contract_tables(gathered, tables)
    return (fresh[None, None], coeffs[None, None])


def solution(mesh):
    placed = (
        P(None, "sec", None, "lat", "col"),
        P(None, "sec", None, "lat", "col"),
        P(None, None, None, ("sec", "lat"), "col", None),
        P("col", "lat", None),
        P(),
    )
    return jax.shard_map(
        shards,
        mesh=mesh,
        in_specs=placed,
        out_specs=(P(None, "sec", None, "lat", "col"), P("sec", None, "col", "lat", None, None)),
        check_vma=False,
    )
```

```python
import math

import jax
import jax.numpy as jnp
from jax import lax
from jax.experimental import pallas as pl
from jax.experimental.pallas import tpu as pltpu
from jax.sharding import PartitionSpec as P

NLON = 384
NLAT = 192
MMAX = 128
NSUB = 4
LANES = 128
ROWS = 8

COURANT_SCALE = 0.4
CONDENSE = 0.5


def permute_kernel(x_ref, order_ref, out_ref, parts, held):
    levels = x_ref.shape[-2]
    rows = held.shape[0]
    cols = order_ref.shape[1]
    tiles = cols // LANES
    gathered = held.shape[1] // LANES
    multiplied = tiles - gathered
    halves = 2 if tiles % 2 == 0 else 1
    width = halves * LANES
    fill = jnp.zeros((rows - levels, LANES), jnp.float32)
    groups = range(rows // ROWS)

    for s in range(tiles):
        if x_ref.ndim == 2:
            block = x_ref[:, s * LANES : (s + 1) * LANES]
        else:
            per = x_ref.shape[2] // LANES
            block = x_ref[s // per, :, s % per * LANES : (s % per + 1) * LANES]
        if rows > levels:
            block = jnp.concatenate([block, fill], axis=0)
        if s < multiplied:
            coarse = block.astype(jnp.bfloat16)
            parts[s * rows : (s + 1) * rows, :LANES] = coarse
            parts[s * rows : (s + 1) * rows, LANES:] = (
                block - coarse.astype(jnp.float32)
            ).astype(jnp.bfloat16)
        else:
            held[:, (s - multiplied) * LANES : (s - multiplied + 1) * LANES] = block
    wanted = lax.broadcasted_iota(jnp.int32, (2 * LANES, width), 0) & (LANES - 1)

    def one(t, carry):
        order = order_ref[:, pl.ds(pl.multiple_of(t * width, width), width)]
        lane = order & (LANES - 1)
        chosen = jnp.where(wanted == lane, 1.0, 0.0).astype(jnp.bfloat16)
        moved = jnp.dot(parts[...], chosen, preferred_element_type=jnp.float32)
        for h in range(halves):
            mine = slice(h * LANES, (h + 1) * LANES)
            source = jnp.broadcast_to(order[:, mine] >> 7, (ROWS, LANES))
            lanes = jnp.broadcast_to(lane[:, mine], (ROWS, LANES))
            total = [jnp.zeros((ROWS, LANES), jnp.float32) for _ in groups]
            for s in range(gathered):
                hit = source == multiplied + s
                for r in groups:
                    block = held[r * ROWS : (r + 1) * ROWS, s * LANES : (s + 1) * LANES]
                    total[r] = jnp.where(hit, jnp.take_along_axis(block, lanes, axis=1), total[r])
            for s in range(multiplied):
                hit = source == s
                for r in groups:
                    begin = s * rows + r * ROWS
                    total[r] = jnp.where(hit, moved[begin : begin + ROWS, mine], total[r])
            tile = t * halves + h
            for r in groups:
                end = min((r + 1) * ROWS, levels)
                value = total[r][: end - r * ROWS]
                if out_ref.ndim == 2:
                    at = pl.ds(pl.multiple_of(tile * LANES, LANES), LANES)
                    out_ref[r * ROWS : end, at] = value
                else:
                    per = out_ref.shape[2] // LANES
                    at = pl.ds(pl.multiple_of(tile % per * LANES, LANES), LANES)
                    out_ref[tile // per, r * ROWS : end, at] = value
        return carry

    lax.fori_loop(0, tiles // halves, one, 0)


def permute(values, order, shape):
    levels, tiles = values.shape[-2], order.shape[1] // LANES
    rows = -(-levels // ROWS) * ROWS
    gathered = tiles * 3 // 8
    return pl.pallas_call(
        permute_kernel,
        out_shape=jax.ShapeDtypeStruct(shape, jnp.float32),
        in_specs=[pl.BlockSpec(memory_space=pltpu.VMEM)] * 2,
        out_specs=pl.BlockSpec(memory_space=pltpu.VMEM),
        scratch_shapes=[
            pltpu.VMEM(((tiles - gathered) * rows, 2 * LANES), jnp.bfloat16),
            pltpu.VMEM((rows, gathered * LANES), jnp.float32),
        ],
        name="permute",
    )(values, order)


def cloud_kernel(wind_ref, gap_ref, push_ref, anomaly_ref, rain_ref):
    count, levels, width = anomaly_ref.shape
    scale = CONDENSE / count

    for c0 in range(0, width, LANES):
        c1 = min(c0 + LANES, width)
        for base in range(0, levels, 2 * ROWS):
            top = min(base + 2 * ROWS, levels)
            for r0 in range(base, top, ROWS):
                r1 = min(r0 + ROWS, top)
                courant = COURANT_SCALE * jnp.tanh(wind_ref[r0:r1, c0:c1])
                mixing = 0.2 + 0.5 * jnp.abs(courant)
                ahead = mixing - 0.5 * courant
                back = mixing + 0.5 * courant
                keep = 1.0 - 2.0 * mixing
                push = push_ref[r0:r1, c0:c1]
                start = gap_ref[r0:r1, c0:c1]
                gap = [
                    start
                    + anomaly_ref[n, base:top, c0:c1].astype(jnp.float32)[r0 - base : r1 - base]
                    for n in range(count)
                ]
                rain = [jnp.zeros_like(start) for _ in range(2)]
                for substep in range(NSUB):
                    fresh = []
                    for n in range(count):
                        wet = jnp.maximum(gap[n], 0.0)
                        rain[n % 2] = rain[n % 2] + wet
                        if substep < NSUB - 1:
                            fresh.append(
                                (ahead * gap[(n + 1) % count] + back * gap[n - 1])
                                + (keep * gap[n] + (push - wet))
                            )
                    gap = fresh
                found = scale * (rain[0] + rain[1])
                for copy in range(rain_ref.shape[0]):
                    rain_ref[copy, r0:r1, c0:c1] = found


def cloud_model(arrived, anomaly, sections):
    count, levels, _ = anomaly.shape
    blocks, _, span = arrived.shape
    bands = blocks // sections
    block = LANES if span % LANES == 0 else span
    steps = span // block
    if block < LANES:
        anomaly = anomaly.reshape(count, levels, bands, span).transpose(2, 0, 1, 3)
        moist = pl.BlockSpec((None, count, levels, span), lambda i: (i, 0, 0, 0))
    else:
        moist = pl.BlockSpec((count, levels, block), lambda i: (0, 0, i))

    def of(field):
        return pl.BlockSpec(
            (None, levels, block), lambda i: (field * bands + i // steps, 0, i % steps)
        )

    found = pl.pallas_call(
        cloud_kernel,
        grid=(bands * steps,),
        out_shape=jax.ShapeDtypeStruct((sections, bands, levels, span), jnp.float32),
        in_specs=[of(0), of(2), of(3), moist],
        out_specs=pl.BlockSpec(
            (sections, None, levels, block), lambda i: (0, i // steps, 0, i % steps)
        ),
        name="cloud",
    )(arrived, arrived, arrived, anomaly)
    return found.reshape(arrived.shape)


def halve(values):
    coarse = values.astype(jnp.bfloat16)
    return coarse, (values - coarse.astype(jnp.float32)).astype(jnp.bfloat16)


def march_kernel(
    grow_ref, retreat_ref, order_ref, zero_ref, cosine_ref, diag_ref, coarse_ref, fine_ref, *tables
):
    slots = order_ref.shape[0]
    halves = len(tables)
    order = order_ref[...]
    grow = grow_ref[...]
    retreat = retreat_ref[...]
    cosine = [cosine_ref[:, h * LANES : (h + 1) * LANES] for h in range(halves)]
    for h in range(halves):
        tables[h][: 2 * slots, :] = jnp.zeros((2 * slots, LANES), jnp.float32)
    group = 8

    def march(g, carry):
        begin = g * group
        held = [
            [
                tables[h][pl.ds(pl.multiple_of((begin + j) * slots, ROWS), slots), :]
                for j in range(2)
            ]
            for h in range(halves)
        ]
        for j in range(group):
            n = begin + j
            index = zero_ref[...] + n
            grow_n = jnp.take_along_axis(grow, index, axis=1)
            retreat_n = jnp.take_along_axis(retreat, index, axis=1)
            first = order == n
            for h in range(halves):
                previous, current = held[h]
                grown = grow_n * (cosine[h] * current - retreat_n * previous)
                fresh = jnp.where(first, diag_ref[:, h * LANES : (h + 1) * LANES], grown)
                tables[h][pl.ds(pl.multiple_of((n + 2) * slots, ROWS), slots), :] = fresh
                held[h] = [current, fresh]
        return carry

    lax.fori_loop(0, MMAX // group, march, 0)

    def sort(g, carry):
        for j in range(4):
            s = g * 4 + j
            for h in range(halves):
                rows = tables[h][pl.ds(2 * slots + s, MMAX, stride=slots), :]
                mine = slice(h * LANES, (h + 1) * LANES)
                coarse_ref[s, :, mine], fine_ref[s, :, mine] = halve(rows)
        return carry

    lax.fori_loop(0, slots // 4, sort, 0)


def contract_kernel(fourier_ref, coarse_ref, fine_ref, out_ref):
    levels, slots, _, _ = out_ref.shape
    bands = fourier_ref.shape[0]
    terms = 2 * levels
    rows = -(-terms // 16) * 16

    def product(left, right):
        return lax.dot_general(
            left, right, (((1,), (1,)), ((), ())), preferred_element_type=jnp.float32
        )

    def contract(g, carry):
        for j in range(4):
            s = g * 4 + j
            found = [fourier_ref[b, pl.ds(s, terms, stride=slots), :] for b in range(bands)]
            found = jnp.concatenate(found, axis=1)
            if rows > terms:
                fill = jnp.zeros((rows - terms, found.shape[1]), jnp.float32)
                found = jnp.concatenate([found, fill], axis=0)
            head, rest = halve(found)
            main = product(jnp.concatenate([head, rest], axis=0), coarse_ref[s])
            total = main[:rows] + main[rows:] + product(head, fine_ref[s])
            for l in range(levels):
                out_ref[l, s] = total[2 * l : 2 * l + 2]
        return carry

    lax.fori_loop(0, slots // 4, contract, 0)


def dft_kernel(x_ref, trig_ref, out_ref):
    blocks, levels, lats, _ = x_ref.shape
    parts, _, _, slots, lanes = out_ref.shape
    count = trig_ref.shape[1]
    waves = [jnp.concatenate(halve(trig_ref[j]), axis=0) for j in range(blocks)]

    def product(left, right):
        return lax.dot_general(
            left, right, (((1,), (1,)), ((), ())), preferred_element_type=jnp.float32
        )

    for first in range(0, levels, 2):
        last = min(first + 2, levels)
        total = None
        for j in range(blocks):
            grid = []
            for l in range(first, last):
                grid.append(x_ref[j, l])
                if lanes > lats:
                    grid.append(jnp.zeros((lanes - lats, x_ref.shape[3]), jnp.float32))
            coarse, fine = halve(jnp.concatenate(grid, axis=0))
            main = product(waves[j], coarse)
            term = main[:count] + main[count:] + product(waves[j][:count], fine)
            total = term if total is None else total + term
        for l in range(first, last):
            mine = total[:, (l - first) * lanes : (l - first + 1) * lanes]
            for p in range(parts):
                for c in range(2):
                    begin = (p * 2 + c) * slots
                    out_ref[p, l, c] = mine[begin : begin + slots]


def dft(regrouped, wave_table, blocks, parts):
    _, lats, lons = regrouped.shape
    levels = regrouped.shape[0] // blocks
    slots = wave_table.shape[0] // parts
    pad = -lats % ROWS
    lanes = -(-lats // LANES) * LANES
    grid = jnp.pad(regrouped, ((0, 0), (0, pad), (0, 0)))
    trig = trig_table(jnp.arange(NLON, dtype=jnp.int32), wave_table)
    trig = trig.reshape(blocks, lons, 2, parts, slots).transpose(0, 3, 2, 4, 1)
    return pl.pallas_call(
        dft_kernel,
        out_shape=jax.ShapeDtypeStruct((parts, levels, 2, slots, lanes), jnp.float32),
        in_specs=[pl.BlockSpec(memory_space=pltpu.VMEM)] * 2,
        out_specs=pl.BlockSpec(memory_space=pltpu.VMEM),
        name="dft",
    )(
        grid.reshape(blocks, levels, lats + pad, lons),
        trig.reshape(blocks, 2 * parts * slots, lons),
    )


def legendre_terms(orders, lats):
    colatitude = (jnp.arange(lats, dtype=jnp.int32).astype(jnp.float32) + 0.5) * (math.pi / lats)
    sine_lat = jnp.sin(colatitude)
    order_col = orders.astype(jnp.float32)[:, None]
    log_diag = 0.5 * (
        lax.lgamma(order_col + 1.5) - lax.lgamma(jnp.float32(1.5)) - lax.lgamma(order_col + 1.0)
    )
    log_diag = log_diag + order_col * jnp.log(sine_lat)[None, :] - 0.5 * math.log(2.0)
    diagonal = jnp.exp(log_diag) * (sine_lat / math.sqrt(lats))[None, :]
    degree = jnp.arange(MMAX, dtype=jnp.int32).astype(jnp.float32)[None, :]
    active = degree > order_col
    numerator = jnp.where(active, 4.0 * degree * degree - 1.0, 0.0)
    bottom = jnp.where(active, degree * degree - order_col * order_col, 1.0)
    lower = degree - 1.0
    retreat = jnp.sqrt(
        jnp.maximum(lower * lower - order_col * order_col, 0.0) / (4.0 * lower * lower - 1.0)
    )
    return jnp.sqrt(numerator / bottom), retreat, jnp.cos(colatitude), diagonal


def legendre_tables(orders, lats, bands):
    slots = orders.shape[0]
    wide = bands * (-(-(lats // bands) // LANES) * LANES)
    grow, retreat, cosine, diagonal = legendre_terms(orders, lats)

    def spread(values):
        cut = values.reshape(values.shape[0], bands, lats // bands)
        cut = jnp.pad(cut, ((0, 0), (0, 0), (0, wide // bands - lats // bands)))
        return cut.reshape(values.shape[0], wide)

    table = jax.ShapeDtypeStruct((slots, MMAX, wide), jnp.bfloat16)
    return pl.pallas_call(
        march_kernel,
        out_shape=[table] * 2,
        in_specs=[pl.BlockSpec(memory_space=pltpu.VMEM)] * 6,
        out_specs=[pl.BlockSpec(memory_space=pltpu.VMEM)] * 2,
        scratch_shapes=[pltpu.VMEM(((MMAX + 2) * slots, LANES), jnp.float32)] * (wide // LANES),
        cost_estimate=pl.CostEstimate(
            flops=6 * MMAX * slots * wide, bytes_accessed=16 * MMAX * slots * wide, transcendentals=0
        ),
        name="march",
    )(
        grow,
        retreat,
        jnp.broadcast_to(orders[:, None], (slots, LANES)),
        jnp.zeros((slots, LANES), jnp.int32),
        spread(cosine[None, :]),
        spread(diagonal),
    )


def contract_tables(fourier, tables):
    bands, levels, _, slots, lanes = fourier.shape
    return pl.pallas_call(
        contract_kernel,
        out_shape=jax.ShapeDtypeStruct((levels, slots, 2, MMAX), jnp.float32),
        in_specs=[pl.BlockSpec(memory_space=pltpu.VMEM)] * 3,
        out_specs=pl.BlockSpec(memory_space=pltpu.VMEM),
        name="contract",
    )(fourier.reshape(bands, levels * 2 * slots, lanes), *tables)


def trig_table(longitudes, wave_numbers):
    phase = (longitudes[:, None] * wave_numbers[None, :] % NLON).astype(jnp.float32) * (
        2.0 * math.pi / NLON
    )
    return jnp.stack((jnp.cos(phase), jnp.sin(phase)), axis=1) / math.sqrt(NLON)


MESH_IDS = pl.DeviceIdType.MESH


def lanes_product(left, right):
    return lax.dot_general(
        left, right, (((1,), (1,)), ((), ())), preferred_element_type=jnp.float32
    )


def march(grow, retreat, order, zero, cosine, diag_ref, table, coarse_ref, fine_ref):
    slots = order.shape[0]
    table[: 2 * slots, :] = jnp.zeros((2 * slots, LANES), jnp.float32)
    group = 8

    def degrees(g, carry):
        begin = g * group
        previous, current = [
            table[pl.ds(pl.multiple_of((begin + j) * slots, ROWS), slots), :] for j in range(2)
        ]
        for j in range(group):
            n = begin + j
            index = zero + n
            grow_n = jnp.take_along_axis(grow, index, axis=1)
            retreat_n = jnp.take_along_axis(retreat, index, axis=1)
            grown = grow_n * (cosine * current - retreat_n * previous)
            fresh = jnp.where(order == n, diag_ref[...], grown)
            table[pl.ds(pl.multiple_of((n + 2) * slots, ROWS), slots), :] = fresh
            previous, current = current, fresh
        return carry

    lax.fori_loop(0, MMAX // group, degrees, 0)

    def sort(g, carry):
        for j in range(4):
            s = g * 4 + j
            rows = table[pl.ds(2 * slots + s, MMAX, stride=slots), :]
            coarse_ref[s], fine_ref[s] = halve(rows)
        return carry

    lax.fori_loop(0, slots // 4, sort, 0)


def spectral_kernel(
    fresh_ref,
    trig_ref,
    grow_ref,
    retreat_ref,
    order_ref,
    zero_ref,
    cosine_ref,
    diag_ref,
    out_ref,
    zbuf,
    ybuf,
    ystage,
    wave_coarse,
    wave_fine,
    table,
    coarse,
    fine,
    both,
    local_sem,
    zsend,
    zrecv,
    ysend,
    yrecv,
):
    cols = lax.axis_size("col")
    col, lat = lax.axis_index("col"), lax.axis_index("lat")
    levels, lats = zbuf.shape[1], zbuf.shape[2]
    slots = order_ref.shape[0]
    partner = 1 - lat

    barrier = pltpu.get_barrier_semaphore()
    for d in range(1, cols):
        pl.semaphore_signal(
            barrier, inc=1, device_id={"col": lax.rem(col + d, cols)}, device_id_type=MESH_IDS
        )
    pl.semaphore_signal(barrier, inc=1, device_id={"lat": partner}, device_id_type=MESH_IDS)
    own = pltpu.make_async_copy(
        fresh_ref.at[pl.ds(col * levels, levels)], zbuf.at[col], local_sem
    )
    own.start()
    pl.semaphore_wait(barrier, cols)

    def zcopy(l, d):
        dest = lax.rem(col + d, cols)
        return pltpu.make_async_remote_copy(
            src_ref=fresh_ref.at[dest * levels + l],
            dst_ref=zbuf.at[col, l],
            send_sem=zsend.at[l, d - 1],
            recv_sem=zrecv.at[l, d - 1],
            device_id={"col": dest},
            device_id_type=MESH_IDS,
        )

    for l in range(levels):
        for d in range(1, cols):
            zcopy(l, d).start()

    for j in range(cols):
        wave_coarse[j], wave_fine[j] = halve(trig_ref[j])
    march(
        grow_ref[...],
        retreat_ref[...],
        order_ref[...],
        zero_ref[...],
        cosine_ref[...],
        diag_ref,
        table,
        coarse,
        fine,
    )
    own.wait()

    def ycopy(l):
        return pltpu.make_async_remote_copy(
            src_ref=ystage.at[l],
            dst_ref=ybuf.at[lat, l],
            send_sem=ysend.at[l],
            recv_sem=yrecv.at[l],
            device_id={"lat": partner},
            device_id_type=MESH_IDS,
        )

    def transform(l, carry):
        for d in range(1, cols):
            zcopy(l, d).wait_recv()
        total = None
        for j in range(cols):
            head, rest = halve(zbuf[j, l])
            main = lanes_product(jnp.concatenate([head, rest], axis=0), wave_coarse[j])
            term = main[:lats] + main[lats:] + lanes_product(head, wave_fine[j])
            total = term if total is None else total + term
        ybuf[lat, l] = total[:, : 2 * slots]
        ystage[l] = total[:, 2 * slots :]
        ycopy(l).start()
        return carry

    lax.fori_loop(0, levels, transform, 0)

    lane = lax.broadcasted_iota(jnp.int32, (2 * slots, LANES), 1)
    mirror = jnp.where(lane < lats, lats - 1 - lane, lane)
    fill = jnp.zeros((2 * slots, LANES - lats), jnp.float32)
    both[...] = jnp.zeros_like(both)
    span = both.shape[0] // 2

    def mix(l, carry):
        ycopy(l).wait_recv()
        north = jnp.concatenate([ybuf[0, l].T, fill], axis=1)
        south = jnp.concatenate([ybuf[1, l].T, fill], axis=1)
        south = jnp.take_along_axis(south, mirror, axis=1)
        at = pl.ds(pl.multiple_of(l * 2 * slots, ROWS), 2 * slots)
        both[at, :] = north + south
        at = pl.ds(pl.multiple_of(span + l * 2 * slots, ROWS), 2 * slots)
        both[at, :] = north - south
        return carry

    lax.fori_loop(0, levels, mix, 0)
    half = both.shape[0] // slots // 2
    degree = lax.broadcasted_iota(jnp.int32, (half, LANES), 1)

    def contract(g, carry):
        for j in range(4):
            s = g * 4 + j
            head, rest = halve(both[pl.ds(s, 2 * half, stride=slots), :])
            main = lanes_product(jnp.concatenate([head, rest], axis=0), coarse[s])
            total = main[: 2 * half] + main[2 * half :] + lanes_product(head, fine[s])
            even = ((order_ref[pl.ds(s, 1), :] + degree) & 1) == 0
            total = jnp.where(even, total[:half], total[half:])
            for l in range(levels):
                out_ref[l, s] = total[2 * l : 2 * l + 2]
        return carry

    lax.fori_loop(0, slots // 4, contract, 0)

    def drain(l, carry):
        for d in range(1, cols):
            zcopy(l, d).wait_send()
        ycopy(l).wait_send()
        return carry

    lax.fori_loop(0, levels, drain, 0)


def spectral_step(fresh, wave_table):
    cols, lat_bands = lax.axis_size("col"), lax.axis_size("lat")
    total_levels, band_rows, lon_block = fresh.shape
    levels = total_levels // cols
    slots = MMAX // lat_bands
    lat = lax.axis_index("lat")
    waves = lax.dynamic_slice_in_dim(
        jnp.concatenate([wave_table, wave_table]), lat * slots, lat_bands * slots
    )
    trig = trig_table(jnp.arange(NLON, dtype=jnp.int32), waves)
    trig = trig.reshape(cols, lon_block, 2, lat_bands, slots).transpose(0, 3, 2, 4, 1)
    trig = trig.reshape(cols, lat_bands * 2 * slots, lon_block)
    grow, retreat, cosine, diagonal = legendre_terms(waves[:slots], NLAT)
    pad = ((0, 0), (0, LANES - band_rows))
    vmem = pl.BlockSpec(memory_space=pltpu.VMEM)
    half = -(-2 * levels // ROWS) * ROWS
    return pl.pallas_call(
        spectral_kernel,
        out_shape=jax.ShapeDtypeStruct((levels, slots, 2, MMAX), jnp.float32),
        in_specs=[pl.BlockSpec(memory_space=pl.ANY)] + [vmem] * 7,
        out_specs=vmem,
        scratch_shapes=[
            pltpu.VMEM((cols, levels, band_rows, lon_block), jnp.float32),
            pltpu.VMEM((lat_bands, levels, band_rows, 2 * slots), jnp.float32),
            pltpu.VMEM((levels, band_rows, 2 * slots), jnp.float32),
            pltpu.VMEM(trig.shape, jnp.bfloat16),
            pltpu.VMEM(trig.shape, jnp.bfloat16),
            pltpu.VMEM(((MMAX + 2) * slots, LANES), jnp.float32),
            pltpu.VMEM((slots, MMAX, LANES), jnp.bfloat16),
            pltpu.VMEM((slots, MMAX, LANES), jnp.bfloat16),
            pltpu.VMEM((2 * half * slots, LANES), jnp.float32),
            pltpu.SemaphoreType.DMA,
            pltpu.SemaphoreType.DMA((levels, cols - 1)),
            pltpu.SemaphoreType.DMA((levels, cols - 1)),
            pltpu.SemaphoreType.DMA((levels,)),
            pltpu.SemaphoreType.DMA((levels,)),
        ],
        compiler_params=pltpu.CompilerParams(collective_id=1, has_side_effects=True),
        name="spectral",
    )(
        fresh,
        trig,
        grow,
        retreat,
        jnp.broadcast_to(waves[:slots, None], (slots, LANES)),
        jnp.zeros((slots, LANES), jnp.int32),
        jnp.pad(cosine[None, :band_rows], pad),
        jnp.pad(diagonal[:, :band_rows], pad),
    )


GROUP = ROWS
DIGIT = 2 * LANES


def physics_kernel(
    own_ref,
    force_ref,
    anomaly_ref,
    order_ref,
    spread_ref,
    fresh_ref,
    own,
    force,
    mate,
    anomaly,
    parts,
    held,
    onehot,
    stage,
    arrived,
    coef,
    partial,
    rain,
    rain_in,
    grid_sum,
    shared,
    load_sem,
    mate_sem,
    out_send,
    out_recv,
    back_send,
    back_recv,
    share_send,
    share_recv,
):
    sec, lat = lax.axis_index("sec"), lax.axis_index("lat")
    side, core = sec // 2, lax.rem(sec, 2)
    bands = arrived.shape[1]
    rows, span = arrived.shape[2], arrived.shape[3]
    band_rows = fresh_ref.shape[1] and fresh_ref.shape[0] // anomaly.shape[0]
    lon_block = own.shape[1]
    levels, count, _ = anomaly.shape
    groups = rows // GROUP
    depth = levels // groups
    tiles = order_ref.shape[1] // LANES
    per = span // LANES
    gathered = held.shape[1] // LANES
    multiplied = tiles - gathered

    def at(s, b):
        return {"sec": s, "lat": b}

    mate_sec = 2 * side + (1 - core)
    across = 2 * (1 - side) + core
    far = 2 * (1 - side) + (1 - core)

    barrier = pltpu.get_barrier_semaphore()
    for s in (mate_sec, across, far, sec):
        for b in (1 - lat, lat):
            if s is sec and b is lat:
                continue
            pl.semaphore_signal(barrier, inc=1, device_id=at(s, b), device_id_type=MESH_IDS)

    used = levels * band_rows
    loads = [
        pltpu.make_async_copy(own_ref, own.at[pl.ds(0, used)], load_sem.at[0]),
        pltpu.make_async_copy(force_ref, force.at[pl.ds(0, used)], load_sem.at[1]),
        pltpu.make_async_copy(anomaly_ref, anomaly, load_sem.at[2]),
    ]
    for copy in loads:
        copy.start()
    pl.semaphore_wait(barrier, 4 * bands - 1)

    def mate_copy(source):
        return pltpu.make_async_remote_copy(
            src_ref=source,
            dst_ref=mate.at[pl.ds(0, used)],
            send_sem=mate_sem.at[0],
            recv_sem=mate_sem.at[1],
            device_id=at(mate_sec, lat),
            device_id_type=MESH_IDS,
        )

    @pl.when(sec == 2)
    def _():
        mate_copy(force_ref).start()

    @pl.when(sec != 2)
    def _():
        mate_copy(own_ref).start()

    beyond = own.shape[0] - used
    for ref in (own, force, mate):
        ref[used:] = jnp.zeros((beyond, lon_block), jnp.float32)

    digit = lax.broadcasted_iota(jnp.int32, (DIGIT, LANES), 0)

    def mark(t, carry):
        lanes = pl.ds(pl.multiple_of(t * LANES, LANES), LANES)
        low = order_ref[:, lanes] & (DIGIT - 1)
        onehot[:, lanes] = jnp.where(digit == low, 1.0, 0.0).astype(jnp.bfloat16)
        return carry

    lax.fori_loop(0, tiles, mark, 0)
    loads[0].wait()
    loads[1].wait()
    mate_copy(own_ref).wait()

    quad = 4 * lon_block // LANES

    def flatten(q, g):
        found = []
        for v in range(4):
            at_rows = pl.ds(g * band_rows + q * 4 + v, GROUP, stride=groups * band_rows)
            mine, push, other = own[at_rows, :], force[at_rows, :], mate[at_rows, :]
            found.append(
                jnp.where(
                    sec == 3,
                    (push - other) * (1.0 / NSUB),
                    jnp.where(sec == 2, other - mine, mine),
                )
            )
        out = []
        for w in range(quad):
            pieces = []
            for v in range(4):
                lo = max(w * LANES - v * lon_block, 0)
                hi = min((w + 1) * LANES - v * lon_block, lon_block)
                if lo < hi:
                    pieces.append(found[v][:, lo:hi])
            out.append(jnp.concatenate(pieces, axis=1))
        return out

    def split(q, carry):
        for g in range(0, groups, 2):
            for w, pair in enumerate(zip(flatten(q, g), flatten(q, g + 1))):
                block = jnp.concatenate(pair, axis=0)
                base = pl.multiple_of((q * quad + w) * rows + g * GROUP, 2 * GROUP)
                coarse, fine = halve(block)
                parts[pl.ds(base, 2 * GROUP), :LANES] = coarse
                parts[pl.ds(base, 2 * GROUP), LANES:] = fine
        return carry

    def keep_whole(q, carry):
        for g in range(groups):
            for w, block in enumerate(flatten(q, g)):
                lane0 = pl.multiple_of((q * quad + w) * LANES - multiplied * LANES, LANES)
                held[g * GROUP : (g + 1) * GROUP, pl.ds(lane0, LANES)] = block
        return carry

    wanted = lax.broadcasted_iota(jnp.int32, (2 * LANES, 2 * LANES), 0) & (LANES - 1)

    def permute_pair(dest, pair):
        first = dest * bands * per + pair * 2
        order = order_ref[:, pl.ds(pl.multiple_of(first * LANES, LANES), 2 * LANES)]
        lane = order & (LANES - 1)
        chosen = jnp.where(wanted == lane, 1.0, 0.0).astype(jnp.bfloat16)
        moved = jnp.dot(parts[...], chosen, preferred_element_type=jnp.float32)
        for h in range(2):
            mine = slice(h * LANES, (h + 1) * LANES)
            source = jnp.broadcast_to(order[:, mine] >> 7, (ROWS, LANES))
            lanes = jnp.broadcast_to(lane[:, mine], (ROWS, LANES))
            total = [jnp.zeros((ROWS, LANES), jnp.float32) for _ in range(groups)]
            for s in range(gathered):
                hit = source == multiplied + s
                for r in range(groups):
                    block = held[r * ROWS : (r + 1) * ROWS, s * LANES : (s + 1) * LANES]
                    total[r] = jnp.where(hit, jnp.take_along_axis(block, lanes, axis=1), total[r])
            for s in range(multiplied):
                hit = source == s
                for r in range(groups):
                    begin = s * rows + r * ROWS
                    total[r] = jnp.where(hit, moved[begin : begin + ROWS, mine], total[r])
            tile = pair * 2 + h
            to = pl.ds(pl.multiple_of(lax.rem(tile, per) * LANES, LANES), LANES)
            for r in range(groups):
                stage[dest, tile // per, r * ROWS : (r + 1) * ROWS, to] = total[r]

    def out_copy(dest, b):
        return pltpu.make_async_remote_copy(
            src_ref=stage.at[dest, b],
            dst_ref=arrived.at[sec, lat],
            send_sem=out_send.at[dest, b],
            recv_sem=out_recv.at[sec, lat],
            device_id=at(dest, b),
            device_id_type=MESH_IDS,
        )

    def out_local():
        return pltpu.make_async_copy(
            stage.at[sec, lat], arrived.at[sec, lat], out_recv.at[sec, lat]
        )

    @pl.when(sec != 1)
    def _():
        lax.fori_loop(0, multiplied // quad, split, 0)
        lax.fori_loop(multiplied // quad, tiles // quad, keep_whole, 0)
        for dest in (across, far, mate_sec, sec):

            def pairs(p, carry, dest=dest):
                permute_pair(dest, p)
                return carry

            lax.fori_loop(0, bands * per // 2, pairs, 0)
            out_copy(dest, 1 - lat).start()
            if dest is sec:
                out_local().start()
            else:
                out_copy(dest, lat).start()

    for field in (0, 2, 3):
        for b in range(bands):
            pltpu.make_async_copy(
                arrived.at[field, b], arrived.at[field, b], out_recv.at[field, b]
            ).wait()
    loads[2].wait()

    volumes = count // ROWS

    def back_copy(dest, b):
        return pltpu.make_async_remote_copy(
            src_ref=rain.at[dest, b],
            dst_ref=rain_in.at[sec * bands + lat],
            send_sem=back_send.at[dest, b],
            recv_sem=back_recv.at[sec * bands + lat],
            device_id=at(dest, b),
            device_id_type=MESH_IDS,
        )

    def back_local():
        return pltpu.make_async_copy(
            rain.at[sec, lat], rain_in.at[sec * bands + lat], back_recv.at[sec * bands + lat]
        )

    def cloud_group(dest):
        at_rows = pl.ds(pl.multiple_of(dest * GROUP, GROUP), GROUP)
        for b in range(bands):
            for c in range(per):
                lanes = slice(c * LANES, (c + 1) * LANES)
                courant = COURANT_SCALE * jnp.tanh(arrived[0, b, at_rows, lanes])
                mixing = 0.2 + 0.5 * jnp.abs(courant)
                coef[0, b, c] = mixing - 0.5 * courant
                coef[1, b, c] = mixing + 0.5 * courant
                coef[2, b, c] = 1.0 - 2.0 * mixing
                coef[3, b, c] = -arrived[2, b, at_rows, lanes]
                coef[4, b, c] = -arrived[3, b, at_rows, lanes]

        def level(r, carry):
            for b in range(bands):
                moist = jnp.dot(
                    spread_ref[...],
                    anomaly[r * groups + dest, :, b * span : (b + 1) * span],
                    preferred_element_type=jnp.float32,
                )
                for c in range(per):
                    lanes = slice(c * LANES, (c + 1) * LANES)
                    ahead, back, keep, low, push = [
                        coef[k, b, c, pl.ds(r, ROWS, stride=0), :] for k in range(5)
                    ]
                    start = [moist[v * ROWS : (v + 1) * ROWS, lanes] for v in range(volumes)]
                    gap = start
                    for substep in range(NSUB - 1):
                        after = gap[1:] + [pltpu.roll(gap[0], ROWS - 1, axis=0)]
                        before = [pltpu.roll(gap[-1], 1, axis=0)] + gap[:-1]
                        gap = [
                            (ahead * n + back * p) + (keep * x - jnp.maximum(x, low))
                            for n, p, x in zip(after, before, gap)
                        ]
                        low = push
                    total = None
                    for x, y in zip(start, gap):
                        term = x - jnp.minimum(y, push)
                        total = term if total is None else total + term
                    partial[b, pl.ds(pl.multiple_of(r * ROWS, ROWS), ROWS), lanes] = total
            return carry

        lax.fori_loop(0, depth, level, 0)
        row = lax.broadcasted_iota(jnp.int32, (ROWS, LANES), 0)
        for b in range(bands):
            for c in range(per):
                lanes = slice(c * LANES, (c + 1) * LANES)
                found = -count * (coef[3, b, c] + (NSUB - 2) * coef[4, b, c])
                for r in range(depth):
                    sums = jnp.sum(partial[b, r * ROWS : (r + 1) * ROWS, lanes], axis=0, keepdims=True)
                    found = jnp.where(row == r, found + sums, found)
                rain[dest, b, :, lanes] = (CONDENSE / count) * found

    for dest in (across, far, mate_sec, sec):
        cloud_group(dest)
        back_copy(dest, 1 - lat).start()
        if dest is sec:
            back_local().start()
        else:
            back_copy(dest, lat).start()

    sources = rain_in.shape[0]
    for k in range(sources):
        pltpu.make_async_copy(rain_in.at[k], rain_in.at[k], back_recv.at[k]).wait()

    digits = tiles * LANES // DIGIT
    grid_sum[...] = jnp.zeros_like(grid_sum)
    chunk = 3 * LANES

    def scatter(k, carry):
        halves = []
        for w in range(chunk // LANES):
            tile = k * (chunk // LANES) + w
            at_lanes = pl.ds(pl.multiple_of(lax.rem(tile, per) * LANES, LANES), LANES)
            coarse, fine = halve(rain_in[tile // per, :, at_lanes])
            both = jnp.concatenate([coarse, fine], axis=0)
            high = order_ref[:, pl.ds(pl.multiple_of(tile * LANES, LANES), LANES)] // DIGIT
            high = jnp.broadcast_to(high.astype(jnp.bfloat16), both.shape)
            halves.append(
                jnp.concatenate(
                    [jnp.where(high == d, both, jnp.bfloat16(0)) for d in range(digits)], axis=0
                )
            )
        left = jnp.concatenate(halves, axis=1)
        right = onehot[:, pl.ds(pl.multiple_of(k * chunk, LANES), chunk)]
        grid_sum[...] += lanes_product(left, right)
        return carry

    lax.fori_loop(0, tiles * LANES // chunk, scatter, 0)

    for d in range(digits):
        found = grid_sum[d * 2 * ROWS : d * 2 * ROWS + ROWS] + grid_sum[
            d * 2 * ROWS + ROWS : (d + 1) * 2 * ROWS
        ]
        for h in range(DIGIT // LANES):
            tile = d * (DIGIT // LANES) + h
            shared[sec, tile * ROWS : (tile + 1) * ROWS] = found[:, h * LANES : (h + 1) * LANES]

    def share_copy(kind, group, dest):
        return pltpu.make_async_remote_copy(
            src_ref=shared.at[group],
            dst_ref=shared.at[group],
            send_sem=share_send.at[kind],
            recv_sem=share_recv.at[kind],
            device_id=at(dest, lat),
            device_id_type=MESH_IDS,
        )

    share_copy(0, sec, across).start()
    share_copy(1, sec, mate_sec).start()

    def update(group):
        def one(r, carry):
            base = (r * groups + group) * band_rows
            for q in range(0, band_rows // 4, ROWS):
                pieces = [
                    shared[group, pl.ds((q * quad + w) * ROWS + r, ROWS, stride=quad * ROWS), :]
                    for w in range(quad)
                ]
                for v in range(4):
                    cut = []
                    for w in range(quad):
                        lo = max(v * lon_block - w * LANES, 0)
                        hi = min((v + 1) * lon_block - w * LANES, LANES)
                        if lo < hi:
                            cut.append(pieces[w][:, lo:hi])
                    found = cut[0] if len(cut) == 1 else jnp.concatenate(cut, axis=1)
                    at_rows = pl.ds(base + q * 4 + v, ROWS, stride=4)
                    mine = own[at_rows, :]
                    share = jnp.where(
                        sec < 2,
                        mine * (-1.0 / NSUB),
                        jnp.where(sec == 2, jnp.float32(1), jnp.float32(-1)),
                    )
                    fresh_ref[at_rows, :] = mine + (share * found + force[at_rows, :])
            return carry

        lax.fori_loop(0, depth, one, 0)

    update(sec)
    share_copy(1, mate_sec, mate_sec).wait_recv()
    update(mate_sec)
    share_copy(0, across, across).wait_recv()
    share_copy(2, across, mate_sec).start()
    update(across)
    share_copy(2, far, mate_sec).wait_recv()
    update(far)

    share_copy(0, sec, across).wait_send()
    share_copy(1, sec, mate_sec).wait_send()
    share_copy(2, across, mate_sec).wait_send()
    for dest in (across, far, mate_sec, sec):
        for b in (1 - lat, lat):
            if dest is sec and b is lat:
                continue
            back_copy(dest, b).wait_send()

            @pl.when(sec != 1)
            def _(dest=dest, b=b):
                out_copy(dest, b).wait_send()


def physics_step(own, force, anomaly, order):
    levels, band_rows, lon_block = own.shape
    _, count, width = anomaly.shape
    sections, bands = lax.axis_size("sec"), lax.axis_size("lat")
    tiles = order.shape[0] // LANES
    span = width // bands
    rows = GROUP * sections
    gathered = tiles * 3 // 8
    volumes = count // ROWS
    index = jnp.arange(count, dtype=jnp.int32)
    spread = (index % ROWS * volumes + index // ROWS)[:, None] == index[None, :]
    flat = (levels * band_rows, lon_block)
    padded = (rows * band_rows, lon_block)
    anywhere = pl.BlockSpec(memory_space=pl.ANY)
    vmem = pl.BlockSpec(memory_space=pltpu.VMEM)
    f32, bf16 = jnp.float32, jnp.bfloat16
    fresh = pl.pallas_call(
        physics_kernel,
        out_shape=jax.ShapeDtypeStruct(flat, f32),
        in_specs=[anywhere] * 3 + [vmem] * 2,
        out_specs=vmem,
        scratch_shapes=[
            pltpu.VMEM(padded, f32),
            pltpu.VMEM(padded, f32),
            pltpu.VMEM(padded, f32),
            pltpu.VMEM(anomaly.shape, bf16),
            pltpu.VMEM(((tiles - gathered) * rows, 2 * LANES), bf16),
            pltpu.VMEM((rows, gathered * LANES), f32),
            pltpu.VMEM((DIGIT, tiles * LANES), bf16),
            pltpu.VMEM((sections, bands, rows, span), f32),
            pltpu.VMEM((sections, bands, rows, span), f32),
            pltpu.VMEM((5, bands, span // LANES, GROUP, LANES), f32),
            pltpu.VMEM((bands, levels // sections * ROWS, span), f32),
            pltpu.VMEM((sections, bands, GROUP, span), f32),
            pltpu.VMEM((sections * bands, GROUP, span), f32),
            pltpu.VMEM((tiles * LANES // DIGIT * 2 * GROUP, DIGIT), f32),
            pltpu.VMEM((sections, tiles * GROUP, LANES), f32),
            pltpu.SemaphoreType.DMA((3,)),
            pltpu.SemaphoreType.DMA((2,)),
            pltpu.SemaphoreType.DMA((sections, bands)),
            pltpu.SemaphoreType.DMA((sections, bands)),
            pltpu.SemaphoreType.DMA((sections, bands)),
            pltpu.SemaphoreType.DMA((sections * bands,)),
            pltpu.SemaphoreType.DMA((3,)),
            pltpu.SemaphoreType.DMA((3,)),
        ],
        compiler_params=pltpu.CompilerParams(collective_id=0, has_side_effects=True),
        name="physics",
    )(own.reshape(flat), force.reshape(flat), anomaly, order[None, :], spread.astype(bf16))
    return fresh.reshape(own.shape)


def inverse_order(order):
    cols = order.shape[0]
    tiles = cols // LANES
    slots = jnp.arange(cols, dtype=jnp.int32)
    high = (order[None, :] // LANES) == jnp.arange(tiles, dtype=jnp.int32)[:, None]
    low = (order[:, None] % LANES) == jnp.arange(LANES, dtype=jnp.int32)[None, :]
    digits = jnp.stack((slots // LANES, slots % LANES)).astype(jnp.bfloat16)
    left = jnp.where(high[None], digits[:, None, :], jnp.bfloat16(0)).reshape(2 * tiles, cols)
    found = jnp.dot(left, low.astype(jnp.bfloat16), preferred_element_type=jnp.float32)
    found = found.reshape(2, cols).astype(jnp.int32)
    return found[0] * LANES + found[1]


def shards(state, forcing, crm_moisture, cloud_order, wave_table):
    members, _, levels, band_rows, lon_block = state.shape
    sections = lax.axis_size("sec")
    lat_bands = lax.axis_size("lat")
    block_cols = band_rows * lon_block
    targets = sections * lat_bands
    per_target = block_cols // targets
    field = lax.axis_index("sec")
    slot_list = cloud_order[0, 0]
    own, force = state[0, 0], forcing[0, 0]

    aligned = per_target % LANES == 0 and (block_cols // LANES) % 24 == 0
    grouped = sections == 4 and levels % sections == 0 and levels // sections <= GROUP
    squared = band_rows % 32 == 0 and 4 * lon_block % LANES == 0 and crm_moisture.shape[1] % ROWS == 0
    if lat_bands == 2 and aligned and grouped and squared and NSUB > 2:
        moisture = crm_moisture[0, :, :, 0, 0, :].transpose(1, 0, 2)
        fresh = physics_step(own, force, moisture, slot_list)
        coeffs = spectral_step(fresh, wave_table)
        return (fresh[None, None], coeffs[None, None])

    mate = lax.ppermute(jnp.where(field == 2, force, own), "sec", [(2, 3), (3, 2)])
    part = jnp.where(
        field == 3, (force - mate) / NSUB, jnp.where(field == 2, mate - own, own)
    )
    flat = part.reshape(levels, block_cols)
    cut = (targets, levels, per_target)
    tiled = per_target % LANES == 0
    if tiled:
        outgoing = permute(flat, slot_list[None, :], cut)
    else:
        in_slots = permute(flat, slot_list[None, :], flat.shape)
        outgoing = in_slots.reshape(levels, targets, per_target).transpose(1, 0, 2)
    crm_moisture, outgoing = lax.optimization_barrier((crm_moisture, outgoing))
    arrived = lax.all_to_all(outgoing, ("sec", "lat"), split_axis=0, concat_axis=0, tiled=True)
    homeward = cloud_model(arrived, crm_moisture[0, :, :, 0, 0, :], sections)
    returned = lax.all_to_all(homeward, ("sec", "lat"), split_axis=0, concat_axis=0, tiled=True)
    if not tiled:
        returned = returned.transpose(1, 0, 2).reshape(levels, block_cols)
    rainfall = permute(returned, inverse_order(slot_list)[None, :], flat.shape)
    rainfall = rainfall.reshape(levels, band_rows, lon_block)
    share = jnp.where(
        field < 2, own * (-1.0 / NSUB), jnp.where(field == 2, jnp.float32(1), jnp.float32(-1))
    )
    fresh = own + (share * rainfall + force)

    whole_lanes = 2 * MMAX // lat_bands == LANES and band_rows <= LANES
    if lat_bands == 2 and whole_lanes and levels % lax.axis_size("col") == 0:
        coeffs = spectral_step(fresh, wave_table)
        return (fresh[None, None], coeffs[None, None])

    regrouped = lax.all_to_all(fresh, "col", split_axis=0, concat_axis=0, tiled=True)
    owner_count = MMAX // lat_bands
    wave_table, _ = lax.optimization_barrier((wave_table, rainfall))
    owned_waves = lax.dynamic_slice_in_dim(
        wave_table, lax.axis_index("lat") * owner_count, owner_count
    )
    tables = legendre_tables(owned_waves, NLAT, lat_bands)
    regrouped, tables = lax.optimization_barrier((regrouped, tables))
    spectra = dft(regrouped, wave_table, lax.axis_size("col"), lat_bands)
    gathered = lax.all_to_all(spectra, "lat", split_axis=0, concat_axis=0, tiled=True)
    coeffs = contract_tables(gathered, tables)
    return (fresh[None, None], coeffs[None, None])


def solution(mesh):
    placed = (
        P(None, "sec", None, "lat", "col"),
        P(None, "sec", None, "lat", "col"),
        P(None, None, None, ("sec", "lat"), "col", None),
        P("col", "lat", None),
        P(),
    )
    return jax.shard_map(
        shards,
        mesh=mesh,
        in_specs=placed,
        out_specs=(P(None, "sec", None, "lat", "col"), P("sec", None, "col", "lat", None, None)),
        check_vma=False,
    )
```
